32 devices in a mesh: det: 4 (over y, x), obs: 8 (over z, core).
Axes of the slice: x: 2, y: 2, z: 4, core: 2. Of those that a mesh axis runs over, the one named last changes fastest.
Arguments:
- tod: float32 [4, 8, 8192], P('det', 'obs'), may hold values from -200 to 200
- angle: float32 [4, 8, 8192], P('det', 'obs'), may hold values from -3.140625 to 3.140625
- pix_in: int32 [4, 8, 8192], P('det', 'obs'), may hold values from 0 to 63
- tile_block: int32 [4, 8, 32], P('det', 'obs'), may hold values from 0 to 511
- base_len: int32 [4, 8, 40], P('det', 'obs'), may hold values from 1 to 384, 8192 in all within a row
- touched: int32 [8, 16], P('obs'), may hold values from 0 to 511, as said below
Outputs:
- baselines: float32 [4, 8, 40], P('det', 'obs')
- residual_rate: float32 [4, 8, 40], P('det', 'obs')
The draws below stay inside these ranges and needn't reach their ends.
Inputs may be any that keep to these rules, and one draw needn't show every extreme that they name: `touched`: each row lists 16 distinct patches; patch p is held by owner p // 64; at most 4 patches of one row share an owner, and one owner holds exactly 4 patches of every row.
All inputs are finite; a program needn't handle non-finite values.
Results may differ from the reference program's by a relative error of at most 0.0003.
Values sent between devices are 32-bit elements; how exact they have to be, the bound alone decides.
A program may use at most 128 MiB of HBM per device.

```python
import math
import jax
import jax.numpy as jnp
import numpy as np
from jax import lax

TILE = 256
BLK = 64
PATCH_PIX = 2048
BLOCKS = 32
PT = 16
PATCH_OWN = 64
SAMP = 8192
NTILE = 32
NBASE = 40
BASE_MOST = 384
ITERS = 2
N_DET = 4
N_OBS = 8


def draw_tod(key, part):
    keys = jax.random.split(key, 2)
    ntile = SAMP // TILE
    obs_pos = jnp.arange(N_OBS, dtype=jnp.float32) / max(N_OBS - 1, 1)
    det_pos = jnp.arange(N_DET, dtype=jnp.float32) / max(N_DET - 1, 1)
    level = 3.0 * jnp.exp(jnp.log(3.0) * obs_pos)[None, :, None] * (1.0 + 0.5 * det_pos)[:, None, None]
    white = jnp.clip(jax.random.normal(keys[0], (N_DET, N_OBS, SAMP), jnp.float32), -5.0, 5.0)
    drift = 1.5 * jnp.clip(jax.random.normal(keys[1], (N_DET, N_OBS, ntile), jnp.float32), -6.0, 6.0)
    return level * (white + jnp.repeat(drift, TILE, axis=2))


def draw_touched(key, part):
    keys = jax.random.split(key, 4)
    hot = jax.random.randint(keys[0], (), 0, N_OBS)
    cap = max(2, 2 * PT // N_OBS)
    candidates = (N_OBS - 1) * cap
    rest = PT - cap
    rank_of = jnp.arange(candidates, dtype=jnp.int32) // cap
    copy_of = jnp.arange(candidates, dtype=jnp.int32) % cap
    other = rank_of + (rank_of >= hot).astype(jnp.int32)
    row_keys = jax.random.split(keys[1], N_OBS)
    picks = jax.vmap(lambda row_key: jax.random.permutation(row_key, candidates)[:rest])(row_keys)
    owners = jnp.concatenate([jnp.zeros((N_OBS, cap), jnp.int32) + hot, other[picks]], axis=1)
    copies = jnp.concatenate([jnp.broadcast_to(jnp.arange(cap, dtype=jnp.int32), (N_OBS, cap)), copy_of[picks]], axis=1)
    base = jax.random.randint(keys[2], (N_OBS, N_OBS), 0, PATCH_OWN)
    start = jnp.take_along_axis(base, owners, axis=1)
    sky_regions = owners * PATCH_OWN + (start + copies) % PATCH_OWN
    order_keys = jax.random.split(keys[3], N_OBS)
    order = jax.vmap(lambda row_key: jax.random.permutation(row_key, PT))(order_keys)
    return jnp.take_along_axis(sky_regions, order, axis=1).astype(jnp.int32)


def touch_ends(values, key, least, largest):
    shape = values.shape
    spot = [jax.random.randint(jax.random.fold_in(key, axis), (), 0, shape[axis]) for axis in range(len(shape))]
    values = values.at[tuple(spot)].set(least)
    longest = shape.index(max(shape))
    spot[longest] = (spot[longest] + 1) % shape[longest]
    return values.at[tuple(spot)].set(largest)


def profile(number_of, total, most, lean):
    loads = [(1 << 20) // math.isqrt(grade ** lean) + 1 for grade in range(2, number_of + 1)]
    spare, given = total - most - (number_of - 1), [1] * (number_of - 1)
    while spare > 0:
        movable = [i for i in range(number_of - 1) if given[i] < most]
        whole, budget = sum([loads[i] for i in movable]), spare
        for i in movable:
            extra = min(most - given[i], max(1, budget * loads[i] // whole), spare)
            given[i] = given[i] + extra
            spare = spare - extra
    return np.array([most] + given)


def uneven_parts(own_key, amount, total, most, lean):
    if amount == 2:
        one = jax.random.randint(own_key, (), max(1, total - most), min(most, total - 1) + 1)
        return jnp.stack([one, total - one])
    lengths = jnp.asarray(profile(amount, total, most, lean), jnp.int32)
    twos = (amount - 1) // 2
    donor, taker = lengths[1:1 + 2 * twos:2], lengths[2:2 + 2 * twos:2]
    margin = jnp.minimum(donor - 1, most - taker)
    moved = jax.random.randint(jax.random.fold_in(own_key, 1), (twos,), 0, 1 << 20) % (margin + 1)
    lengths = lengths.at[1:1 + 2 * twos:2].set(donor - moved).at[2:2 + 2 * twos:2].set(taker + moved)
    return lengths[jax.random.permutation(jax.random.fold_in(own_key, 2), amount)]


def setup_inputs(seed: int = 0) -> dict:
    key_list = jax.random.split(jax.random.key(seed), 7)
    return {
        "tod": draw_tod(jax.random.fold_in(key_list[6], 71), 0),
        "angle": jnp.clip(jax.random.uniform(key_list[1], (N_DET, N_OBS, SAMP), jnp.float32, -3.140625, 3.140625), -3.140625, 3.140625),
        "pix_in": touch_ends(jax.random.randint(key_list[2], (N_DET, N_OBS, SAMP), 0, BLK), jax.random.fold_in(key_list[2], 1), 0, BLK - 1).astype(jnp.int32),
        "tile_block": touch_ends(jax.random.randint(key_list[3], (N_DET, N_OBS, NTILE), 0, PT * BLOCKS), jax.random.fold_in(key_list[3], 1), 0, (PT * BLOCKS) - 1).astype(jnp.int32),
        "base_len": jax.vmap(lambda own: uneven_parts(own, NBASE, SAMP, BASE_MOST, 2))(jax.random.split(key_list[4], N_DET * N_OBS)).reshape((N_DET, N_OBS, NBASE)).astype(jnp.int32),
        "touched": draw_touched(jax.random.fold_in(key_list[6], 71), 0),
    }


def pixel_inverse(hits):
    a11 = hits[:, 0] + 1.0
    a12 = hits[:, 1]
    a13 = hits[:, 2]
    a22 = hits[:, 3] + 1.0
    a23 = hits[:, 4]
    a33 = hits[:, 5] + 1.0
    c11 = a22 * a33 - a23 * a23
    c12 = a13 * a23 - a12 * a33
    c13 = a12 * a23 - a13 * a22
    c22 = a11 * a33 - a13 * a13
    c23 = a12 * a13 - a11 * a23
    c33 = a11 * a22 - a12 * a12
    determinant = a11 * c11 + a12 * c12 + a13 * c13
    return jnp.stack([c11, c12, c13, c22, c23, c33], axis=1) / determinant[:, None]


def apply_inverse(inverse, pixel_binned_map):
    first = inverse[:, 0] * pixel_binned_map[:, 0] + inverse[:, 1] * pixel_binned_map[:, 1] + inverse[:, 2] * pixel_binned_map[:, 2]
    second = inverse[:, 1] * pixel_binned_map[:, 0] + inverse[:, 3] * pixel_binned_map[:, 1] + inverse[:, 4] * pixel_binned_map[:, 2]
    third = inverse[:, 2] * pixel_binned_map[:, 0] + inverse[:, 4] * pixel_binned_map[:, 1] + inverse[:, 5] * pixel_binned_map[:, 2]
    return jnp.stack([first, second, third], axis=1)


def column(array, index):
    return lax.dynamic_index_in_dim(array, index, 1, keepdims=False)


def reference(tod, angle, pix_in, tile_block, base_len, touched):
    ndet, nobs, samples = tod.shape
    nbase = base_len.shape[2]
    npix = nobs * PATCH_OWN * PATCH_PIX
    cos_w = jnp.cos(2.0 * angle)
    sin_w = jnp.sin(2.0 * angle)
    tile_of = jnp.arange(samples, dtype=jnp.int32) // TILE
    local = tile_block[:, :, tile_of] * BLK + pix_in
    listed = jnp.broadcast_to(touched[None], (ndet, nobs, touched.shape[1]))
    patch = jnp.take_along_axis(listed, local // PATCH_PIX, axis=2)
    pixel = (patch * PATCH_PIX + local % PATCH_PIX).astype(jnp.int32)
    ends = jnp.cumsum(base_len, axis=2)
    positions = jnp.arange(samples, dtype=jnp.int32)
    base_index = jax.vmap(jax.vmap(lambda edges: jnp.searchsorted(edges, positions, side="right")))(ends).astype(jnp.int32)
    offsets = (jnp.arange(ndet * nobs, dtype=jnp.int32) * nbase).reshape(ndet, nobs, 1)
    flat_index = (base_index + offsets).reshape(-1)

    def baseline_sum(value_entries):
        return jax.ops.segment_sum(value_entries.reshape(-1), flat_index, num_segments=ndet * nobs * nbase).reshape(ndet, nobs, nbase)

    def bin_sky(make_values, comps):
        def add_one(sky, index):
            value_entries = make_values(index).reshape(comps, -1)
            where = column(pixel, index).reshape(-1)
            return sky.at[:, where].add(value_entries), None
        sky, unused = lax.scan(add_one, jnp.zeros((comps, npix), jnp.float32), jnp.arange(nobs, dtype=jnp.int32))
        return sky

    def unbin(sky_map):
        return sky_map[0][pixel] + cos_w * sky_map[1][pixel] + sin_w * sky_map[2][pixel]

    def first_values(index):
        signal = column(tod, index)
        cosine = column(cos_w, index)
        sine = column(sin_w, index)
        return jnp.stack([signal, signal * cosine, signal * sine, jnp.ones_like(signal), cosine, sine, cosine * cosine, cosine * sine, sine * sine])

    sky_first = bin_sky(first_values, 9)
    inverse = pixel_inverse(sky_first[None, 3:])
    start_map = apply_inverse(inverse, sky_first[None, :3])[0]
    right_side = baseline_sum(tod - unbin(start_map))

    def apply_operator(direction):
        expanded = jnp.take_along_axis(direction, base_index, axis=2)

        def values_of(index):
            part = column(expanded, index)
            return jnp.stack([part, part * column(cos_w, index), part * column(sin_w, index)])

        sky = bin_sky(values_of, 3)
        solved = apply_inverse(inverse, sky[None])[0]
        return baseline_sum(expanded - unbin(solved))

    solution = jnp.zeros_like(right_side)
    residual_vector = right_side
    direction = right_side
    norm_now = jnp.sum(residual_vector * residual_vector)
    for step in range(ITERS):
        image = apply_operator(direction)
        alpha = norm_now / jnp.sum(direction * image)
        solution = solution + alpha * direction
        residual_vector = residual_vector - alpha * image
        if step + 1 < ITERS:
            norm_next = jnp.sum(residual_vector * residual_vector)
            direction = residual_vector + (norm_next / norm_now) * direction
            norm_now = norm_next
    return solution, residual_vector / base_len.astype(jnp.float32)
```

```python
import functools

import jax
import jax.numpy as jnp
from jax import lax
from jax.experimental import pallas as pl
from jax.experimental.pallas import tpu as pltpu
from jax.sharding import PartitionSpec as P

TILE = 256
BLK = 64
PATCH_PIX = 2048
LANES = 128
GROUP = 8
MESH = pl.DeviceIdType.MESH
F32 = jnp.float32
BF16 = jnp.bfloat16


def split3(x):
    hi = x.astype(BF16).astype(F32)
    rest = x - hi
    mid = rest.astype(BF16).astype(F32)
    return hi, mid, rest - mid


def eye(n):
    return lax.broadcasted_iota(jnp.int32, (n, n), 0) == lax.broadcasted_iota(jnp.int32, (n, n), 1)


def to_column(row):
    n = row.shape[1]
    return jnp.sum(jnp.where(eye(n), row, 0.0), axis=1, keepdims=True)


def to_row(col):
    n = col.shape[0]
    return jnp.sum(jnp.where(eye(n), col, 0.0), axis=0, keepdims=True)


def total(x):
    return jnp.sum(jnp.sum(x, axis=1, keepdims=True), axis=0, keepdims=True)


def kernel(
    ndet, nobs, tod_ref, angle_ref, pix_ref, tile_ref, len_ref, touched_ref,
    sol_ref, rate_ref,
    g_ref, equal_ref, inv_ref, ids_ref, ball1, ball2, ball3, ball4,
    a_send, a_recv, p_send, p_recv,
):
    n = ndet * nobs
    nchip = n // 2
    nbase = len_ref.shape[1]
    ntile = tile_ref.shape[1]
    patches = touched_ref.shape[1]
    blocks = PATCH_PIX // BLK
    me = lax.axis_index("det") * nobs + lax.axis_index("obs")
    chip = me // 2
    core = me % 2
    slot = core * nchip + chip
    other = 1 - core

    def place(c, k):
        flat = c * 2 + k
        return (flat // nobs, flat % nobs)

    barrier = pltpu.get_barrier_semaphore()

    def greet(r, carry):
        pl.semaphore_signal(
            barrier, inc=1, device_id=place((chip + r) % nchip, core), device_id_type=MESH
        )
        return carry

    lax.fori_loop(1, nchip, greet, 0)
    pl.semaphore_signal(barrier, inc=1, device_id=place(chip, other), device_id_type=MESH)

    def copy_a(ball, s, r, block, target):
        return pltpu.make_async_remote_copy(
            src_ref=ball.at[block], dst_ref=ball.at[block],
            send_sem=a_send.at[s], recv_sem=a_recv.at[s, r],
            device_id=target, device_id_type=MESH,
        )

    def copy_p(ball, s, block):
        return pltpu.make_async_remote_copy(
            src_ref=ball.at[block], dst_ref=ball.at[block],
            send_sem=p_send.at[s], recv_sem=p_recv.at[s],
            device_id=place(chip, other), device_id_type=MESH,
        )

    def start(ball, s):
        def one(r, carry):
            copy_a(ball, s, r, slot, place((chip + r) % nchip, core)).start()
            return carry

        lax.fori_loop(1, nchip, one, 0)
        copy_p(ball, s, slot).start()

    def finish(ball, s):
        def one(r, carry):
            came = core * nchip + (chip - r + nchip) % nchip
            copy_a(ball, s, r, came, place(chip, other)).wait_recv()
            copy_p(ball, s, came).start()
            return carry

        lax.fori_loop(1, nchip, one, 0)
        copy_a(ball, s, 1, pl.ds(0, nchip - 1), place(chip, other)).wait_send()
        copy_p(ball, s, pl.ds(core * nchip, nchip)).wait_send()
        copy_p(ball, s, pl.ds(other * nchip, nchip)).wait_recv()

    tile_row = tile_ref[...]
    patch_of = lax.shift_right_logical(tile_row, blocks.bit_length() - 1)
    block_of = jnp.bitwise_and(tile_row, blocks - 1).astype(F32)
    touched_col = to_column(touched_ref[...].astype(F32))
    chosen = lax.broadcasted_iota(jnp.int32, (patches, ntile), 0) == patch_of
    ids_row = (
        jnp.sum(jnp.where(chosen, touched_col, 0.0), axis=0, keepdims=True) * float(blocks)
        + block_of
    )
    ids_col = to_column(ids_row)
    id_rows = ids_ref.shape[1]
    spot = lax.broadcasted_iota(jnp.int32, (id_rows, LANES), 0) * LANES + lax.broadcasted_iota(
        jnp.int32, (id_rows, LANES), 1
    )
    mine = (spot >= slot * ntile) & (spot < slot * ntile + ntile)
    ids_wide = jnp.concatenate([ids_row] * (LANES // ntile), axis=1)
    ids_ref[slot] = jnp.where(mine, ids_wide, 0.0)

    len_row = len_ref[...].astype(F32)
    len_col = to_column(len_row)
    lower = lax.broadcasted_iota(jnp.int32, (nbase, nbase), 1) <= lax.broadcasted_iota(
        jnp.int32, (nbase, nbase), 0
    )
    ends_f = jnp.sum(jnp.where(lower, len_row, 0.0), axis=1, keepdims=True)
    ends = ends_f.astype(jnp.int32)
    starts = (ends_f - len_col).astype(jnp.int32)

    pl.semaphore_wait(barrier, nchip)
    start(ids_ref, 2)

    pixel = lax.broadcasted_iota(jnp.int32, (BLK, TILE), 0)
    where_in = lax.broadcasted_iota(jnp.int32, (1, TILE), 1)
    per = TILE // LANES

    def build(g, acc):
        at = pl.multiple_of(g * GROUP * per, GROUP * per)
        tod = tod_ref[pl.ds(at, GROUP * per), :]
        angle = angle_ref[pl.ds(at, GROUP * per), :]
        pix = pix_ref[pl.ds(at, GROUP * per), :]
        cw = jnp.cos(2.0 * angle)
        sw = jnp.sin(2.0 * angle)
        c3 = split3(cw)
        s3 = split3(sw)
        parts = [split3(v) for v in (tod, tod * cw, tod * sw, cw * cw, cw * sw)]
        rows = []

        def line(x, i):
            return jnp.concatenate([x[per * i + j : per * i + j + 1] for j in range(per)], axis=1)

        for i in range(GROUP):
            pos = where_in + (g * GROUP + i) * TILE
            ind = (pos >= starts) & (pos < ends)
            tod_line = line(tod, i)
            acc = acc + jnp.where(ind, tod_line, 0.0)
            oh = line(pix, i) == pixel
            pieces = []
            for j in range(3):
                pieces.append(jnp.where(oh, line(c3[j], i), 0.0))
                pieces.append(jnp.where(oh, line(s3[j], i), 0.0))
            pieces.append(jnp.where(oh, 1.0, 0.0))
            rhs = jnp.concatenate(pieces, axis=0).astype(BF16)
            vals = [line(p[j], i) for j in range(3) for p in parts]
            vals.append(jnp.zeros((1, TILE), F32))
            lhs = jnp.concatenate([jnp.where(ind, 1.0, 0.0)] + vals, axis=0).astype(BF16)
            res = lax.dot_general(
                lhs, rhs, (((1,), (1,)), ((), ())), preferred_element_type=F32
            )
            top = res[:nbase]
            cs = top[:, 0:128] + top[:, 128:256] + top[:, 256:384]
            one = jnp.concatenate([top[:, 384:448], jnp.zeros((nbase, BLK), F32)], axis=1)
            gt = jnp.concatenate([cs, one], axis=1)
            g_ref[g * GROUP + i] = gt
            hit = jnp.sum(gt, axis=0, keepdims=True)
            v = res[nbase:, 384:448]
            v = v[0:5] + v[5:10] + v[10:15]
            rows.append(
                jnp.concatenate(
                    [v[1:2], v[2:3], v[0:1], hit[:, 128:192], hit[:, 0:128], v[3:4], v[4:5]],
                    axis=1,
                )
            )
        ball1[slot, pl.ds(pl.multiple_of(g * GROUP, GROUP), GROUP), :] = jnp.concatenate(
            rows, axis=0
        )
        return acc

    acc = lax.fori_loop(0, ntile // GROUP, build, jnp.zeros((nbase, TILE), F32))
    f_tod = jnp.sum(acc, axis=1, keepdims=True)

    start(ball1, 1)
    finish(ids_ref, 2)
    id_table = lax.fori_loop(
        0, n, lambda j, t: t + ids_ref[j], jnp.zeros((id_rows, LANES), F32)
    )
    for q in range(id_rows):
        equal_ref[:, q * LANES : (q + 1) * LANES] = jnp.where(
            ids_col == id_table[q : q + 1, :], 1.0, 0.0
        ).astype(BF16)
    finish(ball1, 1)

    step = TILE // ntile

    def match(ball):
        width = ball.shape[2]

        def one(j, s):
            b = ball[pl.ds(j * step, step)].reshape(TILE, width)
            hi = b.astype(BF16)
            rest = b - hi.astype(F32)
            mid = rest.astype(BF16)
            lo = (rest - mid.astype(F32)).astype(BF16)
            e = equal_ref[:, pl.ds(pl.multiple_of(j * TILE, TILE), TILE)]
            for part in (hi, mid, lo):
                s = s + jnp.dot(e, part, preferred_element_type=F32)
            return s

        return lax.fori_loop(0, n // step, one, jnp.zeros((ntile, width), F32))

    def solve(tc, ts, t):
        m1 = inv_ref[0] * t + inv_ref[1] * tc + inv_ref[2] * ts
        m2 = inv_ref[1] * t + inv_ref[3] * tc + inv_ref[4] * ts
        m3 = inv_ref[2] * t + inv_ref[4] * tc + inv_ref[5] * ts
        return jnp.concatenate([m2, m3, m1, jnp.zeros_like(m1)], axis=1)

    def unbin(m):
        out = jnp.zeros((nbase, 4 * BLK), F32)
        for t in range(ntile):
            out = out + g_ref[t] * m[t : t + 1, :]
        return jnp.sum(out, axis=1, keepdims=True)

    def bin_out(ball, d, scalar):
        pad = lax.broadcasted_iota(jnp.int32, (GROUP, 4 * BLK), 1) >= 3 * BLK
        for g in range(ntile // GROUP):
            rows = [
                jnp.sum(g_ref[g * GROUP + i] * d, axis=0, keepdims=True) for i in range(GROUP)
            ]
            ball[slot, g * GROUP : (g + 1) * GROUP, :] = jnp.where(
                pad, scalar, jnp.concatenate(rows, axis=0)
            )

    def scalar_of(ball):
        s = lax.fori_loop(
            0, n, lambda j, t: t + ball[j, 0:8, 128:256], jnp.zeros((8, LANES), F32)
        )
        return s[0:1, BLK : BLK + 1]

    def apply(ball, d):
        s = match(ball)
        return len_col * d - unbin(solve(s[:, 0:64], s[:, 64:128], s[:, 128:192]))

    s1 = match(ball1)
    a11 = s1[:, 192:256] + 1.0
    a12 = s1[:, 256:320]
    a13 = s1[:, 320:384]
    a22 = s1[:, 384:448] + 1.0
    a23 = s1[:, 448:512]
    a33 = (s1[:, 192:256] - s1[:, 384:448]) + 1.0
    c11 = a22 * a33 - a23 * a23
    c12 = a13 * a23 - a12 * a33
    c13 = a12 * a23 - a13 * a22
    c22 = a11 * a33 - a13 * a13
    c23 = a12 * a13 - a11 * a23
    c33 = a11 * a22 - a12 * a12
    determinant = a11 * c11 + a12 * c12 + a13 * c13
    for i, c in enumerate((c11, c12, c13, c22, c23, c33)):
        inv_ref[i] = c / determinant
    r0 = f_tod - unbin(solve(s1[:, 0:64], s1[:, 64:128], s1[:, 128:192]))

    bin_out(ball2, r0, total(r0 * r0))
    start(ball2, 0)
    finish(ball2, 0)
    rr0 = scalar_of(ball2)
    q0 = apply(ball2, r0)

    bin_out(ball3, q0, total(r0 * q0))
    start(ball3, 1)
    finish(ball3, 1)
    rq = scalar_of(ball3)
    w = apply(ball3, q0)
    alpha0 = rr0 / rq
    r1 = r0 - alpha0 * q0
    z = q0 - alpha0 * w

    lane = lax.broadcasted_iota(jnp.int32, (8, LANES), 1)
    sums = (total(r1 * r1), total(r1 * z), total(r1 * q0) + total(r0 * z))
    packed = jnp.zeros((8, LANES), F32)
    for i, v in enumerate(sums):
        packed = jnp.where(lane == i, v, packed)
    ball4[slot] = packed
    start(ball4, 0)
    finish(ball4, 0)
    got = lax.fori_loop(0, n, lambda j, t: t + ball4[j], jnp.zeros((8, LANES), F32))
    rr1 = got[0:1, 0:1]
    beta = rr1 / rr0
    d1 = r1 + beta * r0
    image = z + beta * q0
    curve = got[0:1, 1:2] + beta * got[0:1, 2:3] + beta * beta * rq
    alpha1 = rr1 / curve
    sol_ref[...] = to_row(alpha0 * r0 + alpha1 * d1)
    rate_ref[...] = to_row((r1 - alpha1 * image) / len_col)


def solution(mesh):
    ndet = mesh.shape["det"]
    nobs = mesh.shape["obs"]
    n = ndet * nobs

    def body(tod, angle, pix_in, tile_block, base_len, touched):
        samples = tod.shape[2]
        ntile = tile_block.shape[2]
        nbase = base_len.shape[2]
        id_rows = n * ntile // LANES
        vmem = pl.BlockSpec(memory_space=pltpu.VMEM)
        sol, rate = pl.pallas_call(
            functools.partial(kernel, ndet, nobs),
            out_shape=[jax.ShapeDtypeStruct((1, nbase), F32)] * 2,
            in_specs=[vmem] * 6,
            out_specs=[vmem] * 2,
            scratch_shapes=[
                pltpu.VMEM((ntile, nbase, 4 * BLK), F32),
                pltpu.VMEM((ntile, n * ntile), BF16),
                pltpu.VMEM((6, ntile, BLK), F32),
                pltpu.VMEM((n, id_rows, LANES), F32),
                pltpu.VMEM((n, ntile, 8 * BLK), F32),
                pltpu.VMEM((n, ntile, 4 * BLK), F32),
                pltpu.VMEM((n, ntile, 4 * BLK), F32),
                pltpu.VMEM((n, 8, LANES), F32),
                pltpu.SemaphoreType.DMA((3,)),
                pltpu.SemaphoreType.DMA((3, n // 2)),
                pltpu.SemaphoreType.DMA((3,)),
                pltpu.SemaphoreType.DMA((3,)),
            ],
            compiler_params=pltpu.CompilerParams(
                collective_id=0, has_side_effects=True, vmem_limit_bytes=60 * 1024 * 1024
            ),
        )(
            tod.reshape(samples // LANES, LANES),
            angle.reshape(samples // LANES, LANES),
            pix_in.reshape(samples // LANES, LANES),
            tile_block.reshape(1, ntile),
            base_len.reshape(1, nbase),
            touched,
        )
        return sol.reshape(1, 1, nbase), rate.reshape(1, 1, nbase)

    spec = P("det", "obs", None)
    return jax.shard_map(
        body,
        mesh=mesh,
        in_specs=(spec, spec, spec, spec, spec, P("obs", None)),
        out_specs=(spec, spec),
        check_vma=False,
    )
```

```python
import functools

import jax
import jax.numpy as jnp
from jax import lax
from jax.experimental import pallas as pl
from jax.experimental.pallas import tpu as pltpu
from jax.sharding import PartitionSpec as P

TILE = 256
BLK = 64
PATCH_PIX = 2048
LANES = 128
GROUP = 8
MESH = pl.DeviceIdType.MESH
F32 = jnp.float32
BF16 = jnp.bfloat16


def split3(x):
    hi = x.astype(BF16).astype(F32)
    rest = x - hi
    mid = rest.astype(BF16).astype(F32)
    return hi, mid, rest - mid


def eye(n):
    return lax.broadcasted_iota(jnp.int32, (n, n), 0) == lax.broadcasted_iota(jnp.int32, (n, n), 1)


def to_column(row):
    n = row.shape[1]
    return jnp.sum(jnp.where(eye(n), row, 0.0), axis=1, keepdims=True)


def to_row(col):
    n = col.shape[0]
    return jnp.sum(jnp.where(eye(n), col, 0.0), axis=0, keepdims=True)


def total(x):
    return jnp.sum(jnp.sum(x, axis=1, keepdims=True), axis=0, keepdims=True)


def kernel(
    ndet, nobs, tod_ref, angle_ref, pix_ref, tile_ref, len_ref, touched_ref,
    out_ref,
    g_ref, equal_ref, inv_ref, ids_ref, ball1, ball2, ball3, ball4,
    a_send, a_recv, p_send, p_recv, d_send, d_recv,
):
    n = ndet * nobs
    nchip = n // 2
    nbase = len_ref.shape[1]
    ntile = tile_ref.shape[1]
    patches = touched_ref.shape[1]
    blocks = PATCH_PIX // BLK
    me = lax.axis_index("det") * nobs + lax.axis_index("obs")
    chip = me // 2
    core = me % 2
    slot = core * nchip + chip
    other = 1 - core

    def place(c, k):
        flat = c * 2 + k
        return (flat // nobs, flat % nobs)

    barrier = pltpu.get_barrier_semaphore()

    def greet(r, carry):
        flat = (me + r) % n
        pl.semaphore_signal(
            barrier, inc=1, device_id=(flat // nobs, flat % nobs), device_id_type=MESH
        )
        return carry

    lax.fori_loop(1, n, greet, 0)

    def copy(ball, block, send, recv, target):
        return pltpu.make_async_remote_copy(
            src_ref=ball.at[block], dst_ref=ball.at[block],
            send_sem=send, recv_sem=recv, device_id=target, device_id_type=MESH,
        )

    def start_direct(ball, s):
        def one(r, carry):
            flat = (me + r) % n
            target = (flat // nobs, flat % nobs)
            copy(ball, slot, d_send.at[s], d_recv.at[s], target).start()
            return carry

        lax.fori_loop(1, n, one, 0)

    def finish_direct(ball, s):
        copy(ball, pl.ds(0, n - 1), d_send.at[s], d_recv.at[s], place(chip, other)).wait()

    det = lax.axis_index("det")
    line = nobs // 2
    spot_z = chip % line
    near = (det + 1 - 2 * (det % 2), (det + 2) % ndet)
    diagonal = (near[0] + 2) % ndet

    def of(d, r):
        return core * nchip + d * line + (spot_z - r + line) % line

    def to_near(k):
        return (near[k], spot_z * 2 + core)

    def partner(ball, s, block):
        return copy(ball, block, p_send.at[s], p_recv.at[s], place(chip, other))

    def share(ball, s, r):
        for k in range(2):
            copy(ball, of(det, r), a_send.at[s], a_recv.at[s, 1 + k, r], to_near(k)).start()
        partner(ball, s, of(det, r)).start()

    def start(ball, s):
        for r in range(1, line):
            target = (det, ((spot_z + r) % line) * 2 + core)
            copy(ball, slot, a_send.at[s], a_recv.at[s, 0, r], target).start()
        share(ball, s, 0)

    def relay(ball, s, r):
        half = ball.shape[1] // 2
        for k in range(2):
            block = of(near[k], r)
            copy(ball, block, a_send.at[s], a_recv.at[s, 1 + k, r], to_near(k)).wait_recv()
            piece = ball.at[block, pl.ds(k * half, half)]
            pltpu.make_async_remote_copy(
                src_ref=piece, dst_ref=piece,
                send_sem=a_send.at[s], recv_sem=a_recv.at[s, 3, r],
                device_id=to_near(1 - k), device_id_type=MESH,
            ).start()
            partner(ball, s, block).start()

    def last(ball, s, r):
        block = of(diagonal, r)
        copy(ball, block, a_send.at[s], a_recv.at[s, 3, r], place(chip, other)).wait_recv()
        partner(ball, s, block).start()

    def finish(ball, s):
        for r in range(line + 2):
            if 0 < r < line:
                copy(
                    ball, of(det, r), a_send.at[s], a_recv.at[s, 0, r], place(chip, other)
                ).wait_recv()
                share(ball, s, r)
            if 1 <= r <= line:
                relay(ball, s, r - 1)
            if 2 <= r:
                last(ball, s, r - 2)
        everyone = place(chip, other)
        copy(ball, pl.ds(0, nchip - 1), a_send.at[s], p_recv.at[s], everyone).wait_send()
        partner(ball, s, pl.ds(core * nchip, nchip)).wait_send()
        partner(ball, s, pl.ds(other * nchip, nchip)).wait_recv()

    tile_row = tile_ref[...]
    patch_of = lax.shift_right_logical(tile_row, blocks.bit_length() - 1)
    block_of = jnp.bitwise_and(tile_row, blocks - 1).astype(F32)
    touched_col = to_column(touched_ref[...].astype(F32))
    chosen = lax.broadcasted_iota(jnp.int32, (patches, ntile), 0) == patch_of
    ids_row = (
        jnp.sum(jnp.where(chosen, touched_col, 0.0), axis=0, keepdims=True) * float(blocks)
        + block_of
    )
    ids_col = to_column(ids_row)
    per_row = LANES // ntile
    id_rows = n // per_row
    lane_row = lax.broadcasted_iota(jnp.int32, (1, LANES), 1) - (slot % per_row) * ntile
    mine = (lane_row >= 0) & (lane_row < ntile)
    ids_ref[slot] = jnp.where(mine, jnp.concatenate([ids_row] * per_row, axis=1), 0.0)

    len_row = len_ref[...].astype(F32)
    len_col = to_column(len_row)
    lower = lax.broadcasted_iota(jnp.int32, (nbase, nbase), 1) <= lax.broadcasted_iota(
        jnp.int32, (nbase, nbase), 0
    )
    ends_f = jnp.sum(jnp.where(lower, len_row, 0.0), axis=1, keepdims=True)
    ends = ends_f.astype(jnp.int32)
    starts = (ends_f - len_col).astype(jnp.int32)

    pl.semaphore_wait(barrier, n - 1)
    start_direct(ids_ref, 0)

    pixel = lax.broadcasted_iota(jnp.int32, (BLK, TILE), 0)
    where_in = lax.broadcasted_iota(jnp.int32, (1, TILE), 1)
    per = TILE // LANES

    def build(g, acc):
        at = pl.multiple_of(g * GROUP * per, GROUP * per)
        tod = tod_ref[pl.ds(at, GROUP * per), :]
        angle = angle_ref[pl.ds(at, GROUP * per), :]
        pix = pix_ref[pl.ds(at, GROUP * per), :]
        cw = jnp.cos(2.0 * angle)
        sw = jnp.sin(2.0 * angle)
        c3 = split3(cw)
        s3 = split3(sw)
        parts = [split3(v) for v in (tod, tod * cw, tod * sw, cw * cw, cw * sw)]
        rows = []

        def strip(x, i):
            return jnp.concatenate([x[per * i + j : per * i + j + 1] for j in range(per)], axis=1)

        for i in range(GROUP):
            pos = where_in + (g * GROUP + i) * TILE
            ind = (pos >= starts) & (pos < ends)
            tod_line = strip(tod, i)
            acc = acc + jnp.where(ind, tod_line, 0.0)
            oh = strip(pix, i) == pixel
            pieces = []
            for j in range(3):
                pieces.append(jnp.where(oh, strip(c3[j], i), 0.0))
                pieces.append(jnp.where(oh, strip(s3[j], i), 0.0))
            pieces.append(jnp.where(oh, 1.0, 0.0))
            rhs = jnp.concatenate(pieces, axis=0).astype(BF16)
            vals = [strip(p[j], i) for j in range(3) for p in parts]
            vals.append(jnp.zeros((1, TILE), F32))
            lhs = jnp.concatenate([jnp.where(ind, 1.0, 0.0)] + vals, axis=0).astype(BF16)
            res = lax.dot_general(
                lhs, rhs, (((1,), (1,)), ((), ())), preferred_element_type=F32
            )
            top = res[:nbase]
            cs = top[:, 0:128] + top[:, 128:256] + top[:, 256:384]
            one = jnp.concatenate([top[:, 384:448], jnp.zeros((nbase, BLK), F32)], axis=1)
            gt = jnp.concatenate([cs, one], axis=1)
            g_ref[g * GROUP + i] = gt
            hit = jnp.sum(gt, axis=0, keepdims=True)
            v = res[nbase:, 384:448]
            v = v[0:5] + v[5:10] + v[10:15]
            rows.append(
                jnp.concatenate(
                    [v[1:2], v[2:3], v[0:1], hit[:, 128:192], hit[:, 0:128], v[3:4], v[4:5]],
                    axis=1,
                )
            )
        ball1[slot, pl.ds(pl.multiple_of(g * GROUP, GROUP), GROUP), :] = jnp.concatenate(
            rows, axis=0
        )
        return acc

    acc = lax.fori_loop(0, ntile // GROUP, build, jnp.zeros((nbase, TILE), F32))
    f_tod = jnp.sum(acc, axis=1, keepdims=True)

    start(ball1, 1)
    finish_direct(ids_ref, 0)
    for q in range(id_rows):
        ids_q = sum(ids_ref[q * per_row + j] for j in range(per_row))
        equal_ref[:, q * LANES : (q + 1) * LANES] = jnp.where(ids_col == ids_q, 1.0, 0.0).astype(
            BF16
        )
    finish(ball1, 1)

    step = TILE // ntile

    def match(ball):
        width = ball.shape[2]

        def one(j, s):
            b = ball[pl.ds(j * step, step)].reshape(TILE, width)
            hi = b.astype(BF16)
            rest = b - hi.astype(F32)
            mid = rest.astype(BF16)
            lo = (rest - mid.astype(F32)).astype(BF16)
            e = equal_ref[:, pl.ds(pl.multiple_of(j * TILE, TILE), TILE)]
            for part in (hi, mid, lo):
                s = s + jnp.dot(e, part, preferred_element_type=F32)
            return s

        return lax.fori_loop(0, n // step, one, jnp.zeros((ntile, width), F32))

    def solve(tc, ts, t):
        m1 = inv_ref[0] * t + inv_ref[1] * tc + inv_ref[2] * ts
        m2 = inv_ref[1] * t + inv_ref[3] * tc + inv_ref[4] * ts
        m3 = inv_ref[2] * t + inv_ref[4] * tc + inv_ref[5] * ts
        return jnp.concatenate([m2, m3, m1, jnp.zeros_like(m1)], axis=1)

    def unbin(m):
        out = jnp.zeros((nbase, 4 * BLK), F32)
        for t in range(ntile):
            out = out + g_ref[t] * m[t : t + 1, :]
        return jnp.sum(out, axis=1, keepdims=True)

    def bin_out(ball, d, scalar):
        pad = lax.broadcasted_iota(jnp.int32, (GROUP, 4 * BLK), 1) >= 3 * BLK
        for g in range(ntile // GROUP):
            rows = [
                jnp.sum(g_ref[g * GROUP + i] * d, axis=0, keepdims=True) for i in range(GROUP)
            ]
            ball[slot, g * GROUP : (g + 1) * GROUP, :] = jnp.where(
                pad, scalar, jnp.concatenate(rows, axis=0)
            )

    def scalar_of(ball):
        s = lax.fori_loop(
            0, n, lambda j, t: t + ball[j, 0:8, 128:256], jnp.zeros((8, LANES), F32)
        )
        return s[0:1, BLK : BLK + 1]

    def apply(ball, d):
        s = match(ball)
        return len_col * d - unbin(solve(s[:, 0:64], s[:, 64:128], s[:, 128:192]))

    s1 = match(ball1)
    a11 = s1[:, 192:256] + 1.0
    a12 = s1[:, 256:320]
    a13 = s1[:, 320:384]
    a22 = s1[:, 384:448] + 1.0
    a23 = s1[:, 448:512]
    a33 = (s1[:, 192:256] - s1[:, 384:448]) + 1.0
    c11 = a22 * a33 - a23 * a23
    c12 = a13 * a23 - a12 * a33
    c13 = a12 * a23 - a13 * a22
    c22 = a11 * a33 - a13 * a13
    c23 = a12 * a13 - a11 * a23
    c33 = a11 * a22 - a12 * a12
    determinant = a11 * c11 + a12 * c12 + a13 * c13
    for i, c in enumerate((c11, c12, c13, c22, c23, c33)):
        inv_ref[i] = c / determinant
    r0 = f_tod - unbin(solve(s1[:, 0:64], s1[:, 64:128], s1[:, 128:192]))

    bin_out(ball2, r0, total(r0 * r0))
    start(ball2, 0)
    finish(ball2, 0)
    rr0 = scalar_of(ball2)
    q0 = apply(ball2, r0)

    bin_out(ball3, q0, total(r0 * q0))
    start(ball3, 1)
    finish(ball3, 1)
    rq = scalar_of(ball3)
    w = apply(ball3, q0)
    alpha0 = rr0 / rq
    r1 = r0 - alpha0 * q0
    z = q0 - alpha0 * w

    lane = lax.broadcasted_iota(jnp.int32, (1, LANES), 1)
    sums = (total(r1 * r1), total(r1 * z), total(r1 * q0) + total(r0 * z))
    packed = jnp.zeros((1, LANES), F32)
    for i, v in enumerate(sums):
        packed = jnp.where(lane == i, v, packed)
    ball4[slot] = packed
    start_direct(ball4, 1)
    finish_direct(ball4, 1)
    got = lax.fori_loop(0, n, lambda j, t: t + ball4[j], jnp.zeros((1, LANES), F32))
    rr1 = got[0:1, 0:1]
    beta = rr1 / rr0
    d1 = r1 + beta * r0
    image = z + beta * q0
    curve = got[0:1, 1:2] + beta * got[0:1, 2:3] + beta * beta * rq
    alpha1 = rr1 / curve
    out_ref[0:1, :] = to_row(alpha0 * r0 + alpha1 * d1)
    out_ref[1:2, :] = to_row((r1 - alpha1 * image) / len_col)


def solution(mesh):
    ndet = mesh.shape["det"]
    nobs = mesh.shape["obs"]
    n = ndet * nobs

    def body(tod, angle, pix_in, tile_block, base_len, touched):
        samples = tod.shape[2]
        ntile = tile_block.shape[2]
        nbase = base_len.shape[2]
        vmem = pl.BlockSpec(memory_space=pltpu.VMEM)
        out = pl.pallas_call(
            functools.partial(kernel, ndet, nobs),
            out_shape=jax.ShapeDtypeStruct((2, nbase), F32),
            in_specs=[vmem] * 6,
            out_specs=vmem,
            scratch_shapes=[
                pltpu.VMEM((ntile, nbase, 4 * BLK), F32),
                pltpu.VMEM((ntile, n * ntile), BF16),
                pltpu.VMEM((6, ntile, BLK), F32),
                pltpu.VMEM((n, 1, LANES), F32),
                pltpu.VMEM((n, ntile, 8 * BLK), F32),
                pltpu.VMEM((n, ntile, 4 * BLK), F32),
                pltpu.VMEM((n, ntile, 4 * BLK), F32),
                pltpu.VMEM((n, 1, LANES), F32),
                pltpu.SemaphoreType.DMA((2,)),
                pltpu.SemaphoreType.DMA((2, 4, nobs // 2)),
                pltpu.SemaphoreType.DMA((2,)),
                pltpu.SemaphoreType.DMA((2,)),
                pltpu.SemaphoreType.DMA((2,)),
                pltpu.SemaphoreType.DMA((2,)),
            ],
            compiler_params=pltpu.CompilerParams(
                collective_id=0, has_side_effects=True, vmem_limit_bytes=60 * 1024 * 1024
            ),
        )(
            tod.reshape(samples // LANES, LANES),
            angle.reshape(samples // LANES, LANES),
            pix_in.reshape(samples // LANES, LANES),
            tile_block.reshape(1, ntile),
            base_len.reshape(1, nbase),
            touched,
        )
        return out[0].reshape(1, 1, nbase), out[1].reshape(1, 1, nbase)

    spec = P("det", "obs", None)
    return jax.shard_map(
        body,
        mesh=mesh,
        in_specs=(spec, spec, spec, spec, spec, P("obs", None)),
        out_specs=(spec, spec),
        check_vma=False,
    )
```

```python
import functools

import jax
import jax.numpy as jnp
from jax import lax
from jax.experimental import pallas as pl
from jax.experimental.pallas import tpu as pltpu
from jax.sharding import PartitionSpec as P

TILE = 256
BLK = 64
PATCH_PIX = 2048
LANES = 128
GROUP = 8
MESH = pl.DeviceIdType.MESH
F32 = jnp.float32
BF16 = jnp.bfloat16


def split3(x):
    hi = x.astype(BF16).astype(F32)
    rest = x - hi
    mid = rest.astype(BF16).astype(F32)
    return hi, mid, rest - mid


def eye(n):
    return lax.broadcasted_iota(jnp.int32, (n, n), 0) == lax.broadcasted_iota(jnp.int32, (n, n), 1)


def to_column(row):
    n = row.shape[1]
    return jnp.sum(jnp.where(eye(n), row, 0.0), axis=1, keepdims=True)


def to_row(col):
    n = col.shape[0]
    return jnp.sum(jnp.where(eye(n), col, 0.0), axis=0, keepdims=True)


def total(x):
    return jnp.sum(jnp.sum(x, axis=1, keepdims=True), axis=0, keepdims=True)


def kernel(
    ndet, nobs, tod_ref, angle_ref, pix_ref, tile_ref, len_ref, touched_ref,
    out_ref,
    g_ref, equal_ref, inv_ref, ids_ref, ball1, ball2, ball3, ball4, sums2, sums3,
    a_send, a_recv, p_send, p_recv, d_send, d_recv,
):
    n = ndet * nobs
    nchip = n // 2
    nbase = len_ref.shape[1]
    ntile = tile_ref.shape[1]
    patches = touched_ref.shape[1]
    blocks = PATCH_PIX // BLK
    me = lax.axis_index("det") * nobs + lax.axis_index("obs")
    chip = me // 2
    core = me % 2
    slot = core * nchip + chip
    other = 1 - core

    def place(c, k):
        flat = c * 2 + k
        return (flat // nobs, flat % nobs)

    barrier = pltpu.get_barrier_semaphore()

    def greet(r, carry):
        flat = (me + r) % n
        pl.semaphore_signal(
            barrier, inc=1, device_id=(flat // nobs, flat % nobs), device_id_type=MESH
        )
        return carry

    lax.fori_loop(1, n, greet, 0)

    def copy(ball, block, send, recv, target):
        return pltpu.make_async_remote_copy(
            src_ref=ball.at[block], dst_ref=ball.at[block],
            send_sem=send, recv_sem=recv, device_id=target, device_id_type=MESH,
        )

    def start_direct(ball, s):
        def one(r, carry):
            flat = (me + r) % n
            target = (flat // nobs, flat % nobs)
            copy(ball, slot, d_send.at[s], d_recv.at[s], target).start()
            return carry

        lax.fori_loop(1, n, one, 0)

    def finish_direct(ball, s):
        copy(ball, pl.ds(0, n - 1), d_send.at[s], d_recv.at[s], place(chip, other)).wait()

    det = lax.axis_index("det")
    line = nobs // 2
    spot_z = chip % line
    near = (det + 1 - 2 * (det % 2), (det + 2) % ndet)
    diagonal = (near[0] + 2) % ndet

    def of(d, r):
        return core * nchip + d * line + (spot_z - r + line) % line

    def to_near(k):
        return (near[k], spot_z * 2 + core)

    def partner(ball, s, block):
        return copy(ball, block, p_send.at[s], p_recv.at[s], place(chip, other))

    def share(ball, s, r):
        for k in range(2):
            copy(ball, of(det, r), a_send.at[s], a_recv.at[s, 1 + k, r], to_near(k)).start()
        partner(ball, s, of(det, r)).start()

    def start(ball, s):
        for r in range(1, line):
            target = (det, ((spot_z + r) % line) * 2 + core)
            copy(ball, slot, a_send.at[s], a_recv.at[s, 0, r], target).start()
        share(ball, s, 0)

    def relay(ball, s, r):
        half = ball.shape[1] // 2
        for k in range(2):
            block = of(near[k], r)
            copy(ball, block, a_send.at[s], a_recv.at[s, 1 + k, r], to_near(k)).wait_recv()
            piece = ball.at[block, pl.ds(k * half, half)]
            pltpu.make_async_remote_copy(
                src_ref=piece, dst_ref=piece,
                send_sem=a_send.at[s], recv_sem=a_recv.at[s, 3, r],
                device_id=to_near(1 - k), device_id_type=MESH,
            ).start()
            partner(ball, s, block).start()

    def last(ball, s, r):
        block = of(diagonal, r)
        copy(ball, block, a_send.at[s], a_recv.at[s, 3, r], place(chip, other)).wait_recv()
        partner(ball, s, block).start()

    def finish(ball, s):
        for r in range(line + 2):
            if 0 < r < line:
                copy(
                    ball, of(det, r), a_send.at[s], a_recv.at[s, 0, r], place(chip, other)
                ).wait_recv()
                share(ball, s, r)
            if 1 <= r <= line:
                relay(ball, s, r - 1)
            if 2 <= r:
                last(ball, s, r - 2)
        everyone = place(chip, other)
        copy(ball, pl.ds(0, nchip - 1), a_send.at[s], p_recv.at[s], everyone).wait_send()
        partner(ball, s, pl.ds(core * nchip, nchip)).wait_send()
        partner(ball, s, pl.ds(other * nchip, nchip)).wait_recv()

    tile_row = tile_ref[...]
    patch_of = lax.shift_right_logical(tile_row, blocks.bit_length() - 1)
    block_of = jnp.bitwise_and(tile_row, blocks - 1).astype(F32)
    touched_col = to_column(touched_ref[...].astype(F32))
    chosen = lax.broadcasted_iota(jnp.int32, (patches, ntile), 0) == patch_of
    ids_row = (
        jnp.sum(jnp.where(chosen, touched_col, 0.0), axis=0, keepdims=True) * float(blocks)
        + block_of
    )
    ids_col = to_column(ids_row)
    per_row = LANES // ntile
    id_rows = n // per_row
    lane_row = lax.broadcasted_iota(jnp.int32, (1, LANES), 1) - (slot % per_row) * ntile
    mine = (lane_row >= 0) & (lane_row < ntile)
    ids_ref[slot] = jnp.where(mine, jnp.concatenate([ids_row] * per_row, axis=1), 0.0)

    len_row = len_ref[...].astype(F32)
    len_col = to_column(len_row)
    lower = lax.broadcasted_iota(jnp.int32, (nbase, nbase), 1) <= lax.broadcasted_iota(
        jnp.int32, (nbase, nbase), 0
    )
    ends_f = jnp.sum(jnp.where(lower, len_row, 0.0), axis=1, keepdims=True)
    ends = ends_f.astype(jnp.int32)
    starts = (ends_f - len_col).astype(jnp.int32)

    pl.semaphore_wait(barrier, n - 1)
    start_direct(ids_ref, 0)

    pixel = lax.broadcasted_iota(jnp.int32, (BLK, TILE), 0)
    where_in = lax.broadcasted_iota(jnp.int32, (1, TILE), 1)
    per = TILE // LANES

    def build(g, acc):
        at = pl.multiple_of(g * GROUP * per, GROUP * per)
        tod = tod_ref[pl.ds(at, GROUP * per), :]
        angle = angle_ref[pl.ds(at, GROUP * per), :]
        pix = pix_ref[pl.ds(at, GROUP * per), :]
        cw = jnp.cos(2.0 * angle)
        sw = jnp.sin(2.0 * angle)
        c3 = split3(cw)
        s3 = split3(sw)
        parts = [split3(v) for v in (tod, tod * cw, tod * sw, cw * cw, cw * sw)]
        rows = []

        def strip(x, i):
            return jnp.concatenate([x[per * i + j : per * i + j + 1] for j in range(per)], axis=1)

        for i in range(GROUP):
            pos = where_in + (g * GROUP + i) * TILE
            ind = (pos >= starts) & (pos < ends)
            tod_line = strip(tod, i)
            acc = acc + jnp.where(ind, tod_line, 0.0)
            oh = strip(pix, i) == pixel
            pieces = []
            for j in range(3):
                pieces.append(jnp.where(oh, strip(c3[j], i), 0.0))
                pieces.append(jnp.where(oh, strip(s3[j], i), 0.0))
            pieces.append(jnp.where(oh, 1.0, 0.0))
            rhs = jnp.concatenate(pieces, axis=0).astype(BF16)
            vals = [strip(p[j], i) for j in range(3) for p in parts]
            vals.append(jnp.zeros((1, TILE), F32))
            lhs = jnp.concatenate([jnp.where(ind, 1.0, 0.0)] + vals, axis=0).astype(BF16)
            res = lax.dot_general(
                lhs, rhs, (((1,), (1,)), ((), ())), preferred_element_type=F32
            )
            top = res[:nbase]
            cs = top[:, 0:128] + top[:, 128:256] + top[:, 256:384]
            one = jnp.concatenate([top[:, 384:448], jnp.zeros((nbase, BLK), F32)], axis=1)
            gt = jnp.concatenate([cs, one], axis=1)
            g_ref[g * GROUP + i] = gt
            hit = jnp.sum(gt, axis=0, keepdims=True)
            v = res[nbase:, 384:448]
            v = v[0:5] + v[5:10] + v[10:15]
            rows.append(
                jnp.concatenate(
                    [v[1:2], v[2:3], v[0:1], hit[:, 128:192], hit[:, 0:128], v[3:4], v[4:5]],
                    axis=1,
                )
            )
        ball1[slot, pl.ds(pl.multiple_of(g * GROUP, GROUP), GROUP), :] = jnp.concatenate(
            rows, axis=0
        )
        return acc

    acc = lax.fori_loop(0, ntile // GROUP, build, jnp.zeros((nbase, TILE), F32))
    f_tod = jnp.sum(acc, axis=1, keepdims=True)

    start(ball1, 1)
    finish_direct(ids_ref, 0)
    for q in range(id_rows):
        ids_q = sum(ids_ref[q * per_row + j] for j in range(per_row))
        equal_ref[:, q * LANES : (q + 1) * LANES] = jnp.where(ids_col == ids_q, 1.0, 0.0).astype(
            BF16
        )
    finish(ball1, 1)

    step = TILE // ntile

    def match(ball):
        width = ball.shape[2]

        packed = width == 2 * BLK
        width = 3 * BLK if packed else width

        def one(j, s):
            b = ball[pl.ds(j * step, step)]
            if packed:
                ones = b[:, ntile:]
                ones = jnp.concatenate([ones[:, :, :BLK], ones[:, :, BLK:]], axis=1)
                b = jnp.concatenate(
                    [b[:, :ntile].reshape(TILE, 2 * BLK), ones.reshape(TILE, BLK)], axis=1
                )
            else:
                b = b.reshape(TILE, width)
            hi = b.astype(BF16)
            rest = b - hi.astype(F32)
            mid = rest.astype(BF16)
            lo = (rest - mid.astype(F32)).astype(BF16)
            e = equal_ref[:, pl.ds(pl.multiple_of(j * TILE, TILE), TILE)]
            for part in (hi, mid, lo):
                s = s + jnp.dot(e, part, preferred_element_type=F32)
            return s

        return lax.fori_loop(0, n // step, one, jnp.zeros((ntile, width), F32))

    def solve(tc, ts, t):
        m1 = inv_ref[0] * t + inv_ref[1] * tc + inv_ref[2] * ts
        m2 = inv_ref[1] * t + inv_ref[3] * tc + inv_ref[4] * ts
        m3 = inv_ref[2] * t + inv_ref[4] * tc + inv_ref[5] * ts
        return jnp.concatenate([m2, m3, m1, jnp.zeros_like(m1)], axis=1)

    def unbin(m):
        out = jnp.zeros((nbase, 4 * BLK), F32)
        for t in range(ntile):
            out = out + g_ref[t] * m[t : t + 1, :]
        return jnp.sum(out, axis=1, keepdims=True)

    def bin_out(ball, scalars, d, scalar):
        scalars[slot] = jnp.broadcast_to(scalar, (1, LANES))
        ones = []
        for g in range(ntile // GROUP):
            rows = jnp.concatenate(
                [jnp.sum(g_ref[g * GROUP + i] * d, axis=0, keepdims=True) for i in range(GROUP)],
                axis=0,
            )
            ball[slot, g * GROUP : (g + 1) * GROUP, :] = rows[:, : 2 * BLK]
            ones.append(rows[:, 2 * BLK : 3 * BLK])
        pairs = len(ones) // 2
        for g in range(pairs):
            ball[slot, ntile + g * GROUP : ntile + (g + 1) * GROUP, :] = jnp.concatenate(
                [ones[g], ones[g + pairs]], axis=1
            )

    def gathered(ball):
        return lax.fori_loop(0, n, lambda j, t: t + ball[j], jnp.zeros((1, LANES), F32))

    def apply(ball, d):
        s = match(ball)
        return len_col * d - unbin(solve(s[:, 0:64], s[:, 64:128], s[:, 128:192]))

    s1 = match(ball1)
    a11 = s1[:, 192:256] + 1.0
    a12 = s1[:, 256:320]
    a13 = s1[:, 320:384]
    a22 = s1[:, 384:448] + 1.0
    a23 = s1[:, 448:512]
    a33 = (s1[:, 192:256] - s1[:, 384:448]) + 1.0
    c11 = a22 * a33 - a23 * a23
    c12 = a13 * a23 - a12 * a33
    c13 = a12 * a23 - a13 * a22
    c22 = a11 * a33 - a13 * a13
    c23 = a12 * a13 - a11 * a23
    c33 = a11 * a22 - a12 * a12
    determinant = a11 * c11 + a12 * c12 + a13 * c13
    for i, c in enumerate((c11, c12, c13, c22, c23, c33)):
        inv_ref[i] = c / determinant
    r0 = f_tod - unbin(solve(s1[:, 0:64], s1[:, 64:128], s1[:, 128:192]))

    bin_out(ball2, sums2, r0, total(r0 * r0))
    start(ball2, 0)
    start_direct(sums2, 2)
    finish(ball2, 0)
    finish_direct(sums2, 2)
    rr0 = gathered(sums2)[:, 0:1]
    q0 = apply(ball2, r0)

    bin_out(ball3, sums3, q0, total(r0 * q0))
    start(ball3, 1)
    start_direct(sums3, 3)
    finish(ball3, 1)
    finish_direct(sums3, 3)
    rq = gathered(sums3)[:, 0:1]
    w = apply(ball3, q0)
    alpha0 = rr0 / rq
    r1 = r0 - alpha0 * q0
    z = q0 - alpha0 * w

    lane = lax.broadcasted_iota(jnp.int32, (1, LANES), 1)
    sums = (total(r1 * r1), total(r1 * z), total(r1 * q0) + total(r0 * z))
    packed = jnp.zeros((1, LANES), F32)
    for i, v in enumerate(sums):
        packed = jnp.where(lane == i, v, packed)
    ball4[slot] = packed
    start_direct(ball4, 1)
    finish_direct(ball4, 1)
    got = gathered(ball4)
    rr1 = got[0:1, 0:1]
    beta = rr1 / rr0
    d1 = r1 + beta * r0
    image = z + beta * q0
    curve = got[0:1, 1:2] + beta * got[0:1, 2:3] + beta * beta * rq
    alpha1 = rr1 / curve
    out_ref[0:1, :] = to_row(alpha0 * r0 + alpha1 * d1)
    out_ref[1:2, :] = to_row((r1 - alpha1 * image) / len_col)


def solution(mesh):
    ndet = mesh.shape["det"]
    nobs = mesh.shape["obs"]
    n = ndet * nobs

    def body(tod, angle, pix_in, tile_block, base_len, touched):
        samples = tod.shape[2]
        ntile = tile_block.shape[2]
        nbase = base_len.shape[2]
        vmem = pl.BlockSpec(memory_space=pltpu.VMEM)
        out = pl.pallas_call(
            functools.partial(kernel, ndet, nobs),
            out_shape=jax.ShapeDtypeStruct((2, nbase), F32),
            in_specs=[vmem] * 6,
            out_specs=vmem,
            scratch_shapes=[
                pltpu.VMEM((ntile, nbase, 4 * BLK), F32),
                pltpu.VMEM((ntile, n * ntile), BF16),
                pltpu.VMEM((6, ntile, BLK), F32),
                pltpu.VMEM((n, 1, LANES), F32),
                pltpu.VMEM((n, ntile, 8 * BLK), F32),
                pltpu.VMEM((n, ntile + ntile // 2, 2 * BLK), F32),
                pltpu.VMEM((n, ntile + ntile // 2, 2 * BLK), F32),
                pltpu.VMEM((n, 1, LANES), F32),
                pltpu.VMEM((n, 1, LANES), F32),
                pltpu.VMEM((n, 1, LANES), F32),
                pltpu.SemaphoreType.DMA((2,)),
                pltpu.SemaphoreType.DMA((2, 4, nobs // 2)),
                pltpu.SemaphoreType.DMA((2,)),
                pltpu.SemaphoreType.DMA((2,)),
                pltpu.SemaphoreType.DMA((4,)),
                pltpu.SemaphoreType.DMA((4,)),
            ],
            compiler_params=pltpu.CompilerParams(
                collective_id=0, has_side_effects=True, vmem_limit_bytes=60 * 1024 * 1024
            ),
        )(
            tod.reshape(samples // LANES, LANES),
            angle.reshape(samples // LANES, LANES),
            pix_in.reshape(samples // LANES, LANES),
            tile_block.reshape(1, ntile),
            base_len.reshape(1, nbase),
            touched,
        )
        return out[0].reshape(1, 1, nbase), out[1].reshape(1, 1, nbase)

    spec = P("det", "obs", None)
    return jax.shard_map(
        body,
        mesh=mesh,
        in_specs=(spec, spec, spec, spec, spec, P("obs", None)),
        out_specs=(spec, spec),
        check_vma=False,
    )
```
